32 devices in a mesh: rep: 8 (over y, x, core), fsdp: 4 (over z).
Axes of the slice: x: 2, y: 2, z: 4, core: 2. Of those that a mesh axis runs over, the one named last changes fastest.
Arguments:
- base: float32 [3, 32, 8192], P(None, 'fsdp'), may hold values from -6 to 6
- local: float32 [8, 3, 32, 8192], P('rep', None, 'fsdp'), may hold values from -6 to 6
- momentum: float32 [3, 32, 8192], P(None, 'fsdp', 'rep'), may hold values from -3 to 3
- hidden: bfloat16 [8, 512, 32], P('rep', 'fsdp'), may hold values from -6 to 6
- out_grad: bfloat16 [8, 512, 8192], P('rep', 'fsdp'), may hold values from -0.06591797 to 0.06591797
Outputs:
- mixed: float32 [8, 3, 32, 8192], P('rep', None, 'fsdp')
- momentum_out: float32 [3, 32, 8192], P(None, 'fsdp', 'rep')
- input_grad: bfloat16 [8, 512, 32], P('rep', 'fsdp')
- weight_grad: float32 [8, 32, 8192], P('rep', 'fsdp')
The draws below stay inside these ranges and needn't reach their ends.
All inputs are finite; a program needn't handle non-finite values.
Results may differ from the reference program's by a relative error of at most 0.015.
Values may be sent and summed in bfloat16 or wider, within the bound.
No kernel may reach another device: no remote copies, remote signals or barrier semaphores. Data moves between devices by JAX's collectives and lax.ppermute only.
A program may use at most 64 MiB of HBM per device.

```python
import jax
import jax.numpy as jnp
from jax import lax

D = 8192
TOK_DEV = 128
REPLICAS = 8
ROWS = 32
TOK_REP = 512
N_FSDP = 4


def steps_of(stream_key, dims, cuts, low, largest):
    loudness, own = 1.0, jax.random.fold_in(stream_key, 6)
    for axis_at, shards_of in cuts:
        steps = jnp.exp(jax.random.uniform(jax.random.fold_in(own, axis_at), (shards_of,), jnp.float32, low / len(cuts), largest / len(cuts)))
        loudness = loudness * jnp.repeat(steps, dims[axis_at] // shards_of).reshape([-1 if axis == axis_at else 1 for axis in range(len(dims))])
    return loudness


def centred(own_key, shape, width, reach, pieces=(), dtype=jnp.bfloat16):
    level = steps_of(own_key, shape, pieces, -0.22, 0.18) if pieces else 1.0
    entries = jax.random.normal(own_key, shape, jnp.float32) * width * level
    return jnp.minimum(jnp.maximum(entries, -reach), reach).astype(dtype)


def setup_inputs(seed: int = 0) -> dict:
    seeds = jax.random.split(jax.random.key(seed), 6)
    base = centred(seeds[0], (3, ROWS, D), 1.0, 6.0, ((1, 4),), jnp.float32)
    local = centred(seeds[1], (REPLICAS, 3, ROWS, D), 1.0, 6.0, ((0, 8), (2, 4)), jnp.float32)
    momentum = centred(seeds[2], (3, ROWS, D), 0.5, 3.0, ((1, 4), (2, 8)), jnp.float32)
    hidden = centred(seeds[3], (REPLICAS, TOK_REP, ROWS), 1.0, 6.0, ((0, 8), (1, 4)))
    out_grad = centred(seeds[4], (REPLICAS, TOK_REP, D), 0.011, 0.06591797, ((0, 8), (1, 4)))
    return {"base": base, "local": local, "momentum": momentum, "hidden": hidden, "out_grad": out_grad}


outer_beta = 0.9
outer_rate = 0.7
mix_keep = 0.5


def reference(base, local, momentum, hidden, out_grad):
    def add_drift(carry, replica):
        return carry + (base - replica), None

    total, _ = lax.scan(add_drift, jnp.zeros_like(base), local)
    delta = total / REPLICAS
    momentum_out = outer_beta * momentum + delta
    updated = base - outer_rate * (delta + outer_beta * momentum_out)
    mixed = mix_keep * local + (1.0 - mix_keep) * updated[None]

    def inner_step(operands):
        params, acts, grads = operands
        weights = params[2].astype(jnp.bfloat16)
        in_grad = jnp.dot(grads, weights.T, preferred_element_type=jnp.float32).astype(jnp.bfloat16)
        act_blocks = acts.reshape(N_FSDP, TOK_DEV, acts.shape[1]).astype(jnp.float32)
        grad_blocks = grads.reshape(N_FSDP, TOK_DEV, grads.shape[1]).astype(jnp.float32)
        partial_value = jnp.einsum("btr,btd->brd", act_blocks, grad_blocks).astype(jnp.bfloat16)
        w_grad = jnp.sum(partial_value.astype(jnp.float32), axis=0)
        return in_grad, w_grad

    input_grad, weight_grad = lax.map(inner_step, (local, hidden, out_grad))
    return mixed, momentum_out, input_grad, weight_grad
```

```python
import jax
import jax.numpy as jnp
from jax import lax
from jax.sharding import PartitionSpec as P

outer_beta = 0.9
outer_rate = 0.7
mix_keep = 0.5


def send(value, axis, target):
    return lax.ppermute(value, axis, [(i, target(i)) for i in range(lax.axis_size(axis))])


def partner(i, k, n):
    return i ^ k if n & (n - 1) == 0 else (i + k) % n


def by_partner(blocks, index, received):
    n = len(blocks)
    if n & (n - 1):
        stack = jnp.stack(blocks)
        shift = [jnp.mod(index - k if received else index + k, n) for k in range(n)]
        return [lax.dynamic_index_in_dim(stack, s, 0, keepdims=False) for s in shift]
    bit = 1
    while bit < n:
        flip = (index & bit) != 0
        blocks = [jnp.where(flip, blocks[k ^ bit], blocks[k]) for k in range(n)]
        bit *= 2
    return blocks


def by_device(blocks, index):
    n = len(blocks)
    if n & (n - 1):
        stack = jnp.stack(blocks)
        return [lax.dynamic_index_in_dim(stack, jnp.mod(index - j, n), 0, keepdims=False) for j in range(n)]
    return by_partner(blocks, index, True)


def per_device(base, local, momentum, hidden, out_grad):
    n_rep, n_f = lax.axis_size("rep"), lax.axis_size("fsdp")
    f, r = lax.axis_index("fsdp"), lax.axis_index("rep")
    mine, grads = local[0], out_grad[0]
    rows = mine.shape[1]
    weights = lax.optimization_barrier(mine[2].astype(jnp.bfloat16))
    wk = [weights] + [send(weights, "fsdp", lambda i: partner(i, k, n_f)) for k in range(1, n_f)]
    a = (1 + outer_beta) / n_rep
    b = outer_beta * outer_beta
    width = momentum.shape[2]
    half = base.shape[2] // 2
    core = r & 1
    term = (base - mine) * a
    own = lax.dynamic_slice_in_dim(term, r * width, width, 2) + b * momentum
    term = lax.dynamic_update_slice_in_dim(term, own, r * width, 2)
    lo, hi = term[:, :, :half], term[:, :, half:]
    total = jnp.where(core == 0, lo, hi)
    give = jnp.where(core == 0, hi, lo).astype(jnp.bfloat16)
    total = total + send(give, "rep", lambda i: i ^ 1).astype(jnp.float32)
    bits = [1 << k for k in range(1, n_rep.bit_length() - 1)]
    for s in range(len(bits)):
        even, odd = bits[s], bits[(s + 1) % len(bits)]
        got = send(total.astype(jnp.bfloat16), "rep", lambda i: i ^ (odd if i & 1 else even))
        total = total + got.astype(jnp.float32)
    got = send(total.astype(jnp.bfloat16), "rep", lambda i: i ^ 1)
    other = got.astype(jnp.float32)
    step = jnp.concatenate([jnp.where(core == 0, total, other), jnp.where(core == 0, other, total)], axis=2)
    mixed = (mix_keep * mine + (1 - mix_keep) * (base - outer_rate * step))[None]
    own_step = lax.dynamic_slice_in_dim(step, r * width, width, 2)
    momentum_out = outer_beta * momentum + (own_step - b * momentum) / (1 + outer_beta)
    hk = hidden[0].reshape(hidden.shape[1], n_f, rows)
    hk = by_partner([hk[:, k] for k in range(n_f)], f, False)
    part = []
    for k in range(n_f):
        part.append(lax.dot_general(hk[k], grads, (((0,), (0,)), ((), ())),
                                    preferred_element_type=jnp.float32).astype(jnp.bfloat16))
    part[0] = lax.optimization_barrier(part[0])
    got = [send(part[k], "fsdp", lambda i: partner(i, k, n_f)) for k in range(1, n_f)]
    weight_grad = part[0][None].astype(jnp.float32)
    for g in got:
        weight_grad = weight_grad + g[None].astype(jnp.float32)
    input_grad = lax.dot_general(grads, jnp.concatenate(wk, axis=0), (((1,), (1,)), ((), ())),
                                 preferred_element_type=jnp.float32).astype(jnp.bfloat16)
    input_grad = by_device([input_grad[:, k * rows:(k + 1) * rows] for k in range(n_f)], f)
    input_grad = jnp.concatenate(input_grad, axis=1)[None]
    return mixed, momentum_out, input_grad, weight_grad


def solution(mesh):
    return jax.shard_map(
        per_device,
        mesh=mesh,
        in_specs=(P(None, "fsdp", None), P("rep", None, "fsdp", None), P(None, "fsdp", "rep"),
                  P("rep", "fsdp", None), P("rep", "fsdp", None)),
        out_specs=(P("rep", None, "fsdp", None), P(None, "fsdp", "rep"), P("rep", "fsdp", None), P("rep", "fsdp", None)),
        check_vma=False,
    )
```
